32 devices in a mesh: sec: 8 (over z, core), env: 4 (over y, x).
Axes of the slice: x: 2, y: 2, z: 4, core: 2. Of those that a mesh axis runs over, the one named last changes fastest.
Arguments:
- env_left: bfloat16 [16, 40, 128, 128], P('sec', None, 'env'), may hold values from -6 to 6
- env_right: bfloat16 [16, 40, 128, 128], P('sec', None, 'env'), may hold values from -6 to 6
- site_left: bfloat16 [1024, 128, 128], P('sec'), may hold values from -0.25 to 0.25
- site_right: bfloat16 [1024, 128, 128], P('sec'), may hold values from -0.25 to 0.25
- source_left: int32 [1024], P('sec'), may hold values from 0 to 15, as said below
- source_right: int32 [1024], P('sec'), may hold values from 0 to 15, as said below
- channel_left: int32 [1024], P('sec'), may hold values from 0 to 7
- channel_right: int32 [1024], P('sec'), may hold values from 0 to 7
- fanin_left: int32 [16], P('sec'), may hold values from 8 to 64, as said below
- fanin_right: int32 [16], P('sec'), may hold values from 8 to 64, as said below
- operator_table: bfloat16 [8, 40, 40], replicated, may hold values from -1.25 to 1.25
- operator_pattern: int32 [8, 40, 40], replicated, may hold values 0 or 1
Outputs:
- new_left: bfloat16 [16, 40, 128, 128], P('sec', None, 'env')
- new_right: bfloat16 [16, 40, 128, 128], P('sec', None, 'env')
The draws below stay inside these ranges and needn't reach their ends.
Inputs may be any that keep to these rules, and one draw needn't show every extreme that they name: `source_left`: among the 128 slots held by one index of sec, all sources owned by one index q of sec (sectors 2 * q to 2 * q + 1) are one and the same sector. `source_right`: among the 128 slots held by one index of sec, all sources owned by one index q of sec are one and the same sector. `fanin_left`: some sector has all 64 slots live. `fanin_right`: some sector has all 64 slots live.
All inputs are finite; a program needn't handle non-finite values.
Results may differ from the reference program's by a relative error of at most 0.015.
Values may be sent and summed in bfloat16 or wider, within the bound.
No kernel may reach another device: no remote copies, remote signals or barrier semaphores. Data moves between devices by JAX's collectives and lax.ppermute only.
A program may use at most 192 MiB of HBM per device.

```python
import jax
import jax.numpy as jnp
from jax import lax

M = 128
W = 40
P_SIZE = 8
SEC_DEV = 2
BLK_SEC = 64
NS = 16
NB = 1024
N_ENV = 4


def sources_for(key, salt):
    owner_count = NS // SEC_DEV
    slot_count = SEC_DEV * BLK_SEC
    base_key = jax.random.fold_in(key, salt)
    key_local, key_used, key_pick = jax.random.split(base_key, 3)
    local_choice = jax.random.randint(key_local, (owner_count, owner_count), 0, SEC_DEV)
    in_use = jax.random.randint(key_used, (owner_count, owner_count), 0, 4) > 0
    in_use = in_use | (jnp.arange(owner_count)[:, None] == jnp.arange(owner_count)[None, :])
    used_count = jnp.sum(in_use.astype(jnp.int32), axis=1)
    picked = jax.random.randint(key_pick, (owner_count, slot_count), 0, used_count[:, None])
    rank_order = jnp.cumsum(in_use.astype(jnp.int32), axis=1) - 1
    matches = in_use[:, None, :] & (rank_order[:, None, :] == picked[:, :, None])
    owners = jnp.sum(matches.astype(jnp.int32) * jnp.arange(owner_count, dtype=jnp.int32)[None, None, :], axis=2)
    local_ids = jnp.take_along_axis(local_choice, owners, axis=1)
    return (owners * SEC_DEV + local_ids).reshape(owner_count * slot_count).astype(jnp.int32)


def fanins_for(key, salt):
    base_key = jax.random.fold_in(key, salt)
    key_level, key_count, key_full = jax.random.split(base_key, 3)
    lowest = BLK_SEC // 8
    levels = jax.random.randint(key_level, (NS,), 0, 3)
    bottom = lowest * jnp.left_shift(jnp.ones((NS,), jnp.int32), levels)
    counts = jax.random.randint(key_count, (NS,), bottom, 2 * bottom + 1)
    full_index = jax.random.randint(key_full, (), 0, NS)
    return jnp.where(jnp.arange(NS) == full_index, BLK_SEC, counts).astype(jnp.int32)


def draw_source_left(key, part):
    return sources_for(key, 11)


def draw_source_right(key, part):
    return sources_for(key, 12)


def draw_fanin_left(key, part):
    return fanins_for(key, 13)


def draw_fanin_right(key, part):
    return fanins_for(key, 14)


def touch_ends(array, key, least, high):
    longest = array.shape.index(max(array.shape))
    spots = []
    for shift in (0, 1):
        where = [jax.random.randint(jax.random.fold_in(key, axis), (), 0, length) for axis, length in enumerate(array.shape)]
        where[longest] = (where[longest] + shift) % array.shape[longest]
        spots.append(tuple(where))
    return array.at[spots[0]].set(least).at[spots[1]].set(high)


def block_scale(own_key, dims, cuts, smallest, top_value):
    factor_of, own = 1.0, jax.random.fold_in(own_key, 6)
    for axis_at, blocks in cuts:
        draws = jnp.exp(jax.random.uniform(jax.random.fold_in(own, axis_at), (blocks,), jnp.float32, smallest / len(cuts), top_value / len(cuts)))
        factor_of = factor_of * jnp.repeat(draws, dims[axis_at] // blocks).reshape([-1 if axis == axis_at else 1 for axis in range(len(dims))])
    return factor_of


def noise(stream_key, extent, spread, bound, shards=(), held_as=jnp.bfloat16):
    result = jax.random.normal(stream_key, extent, jnp.float32) * spread
    if len(shards) > 0:
        result = block_scale(stream_key, extent, shards, -0.22, 0.18) * result
    return jnp.clip(result, min=-bound, max=bound).astype(held_as)


def setup_inputs(seed: int = 0) -> dict:
    arg_keys = jax.random.split(jax.random.key(seed), 13)
    return {
        "env_left": noise(arg_keys[0], (NS, W, M, M), 1.0, 6.0, ((0, 8), (2, 4))),
        "env_right": noise(arg_keys[1], (NS, W, M, M), 1.0, 6.0, ((0, 8), (2, 4))),
        "site_left": noise(arg_keys[2], (NB, M, M), (4 * M) ** -0.5, 0.25, ((0, 8),)),
        "site_right": noise(arg_keys[3], (NB, M, M), (4 * M) ** -0.5, 0.25, ((0, 8),)),
        "source_left": draw_source_left(jax.random.fold_in(arg_keys[12], 71), 0),
        "source_right": draw_source_right(jax.random.fold_in(arg_keys[12], 71), 0),
        "channel_left": touch_ends(jax.random.randint(arg_keys[6], (NB,), 0, P_SIZE), jax.random.fold_in(arg_keys[6], 1), 0, P_SIZE - 1).astype(jnp.int32),
        "channel_right": touch_ends(jax.random.randint(arg_keys[7], (NB,), 0, P_SIZE), jax.random.fold_in(arg_keys[7], 1), 0, P_SIZE - 1).astype(jnp.int32),
        "fanin_left": draw_fanin_left(jax.random.fold_in(arg_keys[12], 71), 0),
        "fanin_right": draw_fanin_right(jax.random.fold_in(arg_keys[12], 71), 0),
        "operator_table": noise(arg_keys[10], (P_SIZE, W, W), (W // 2) ** -0.5, 1.25),
        "operator_pattern": touch_ends((jax.random.randint(arg_keys[11], (P_SIZE, W, W), 0, 2) < 1).astype(jnp.int32), jax.random.fold_in(arg_keys[11], 1), 0, 1),
    }


def side_rebuild(old_tiles, site_blocks, source, channel, fan_in, mixing):
    row_count = M // N_ENV

    def one_sector(sector_index):
        first_slot = sector_index * BLK_SEC
        blocks = lax.dynamic_slice_in_dim(site_blocks, first_slot, BLK_SEC, 0)
        sources = lax.dynamic_slice_in_dim(source, first_slot, BLK_SEC, 0)
        channels = lax.dynamic_slice_in_dim(channel, first_slot, BLK_SEC, 0)
        live_count = lax.dynamic_index_in_dim(fan_in, sector_index, 0, keepdims=False)
        live_mask = jnp.arange(BLK_SEC, dtype=jnp.int32) < live_count
        blocks = jnp.where(live_mask[:, None, None], blocks, jnp.zeros_like(blocks))
        fetched = jnp.take(old_tiles, sources, axis=0)
        mix_slots = jnp.take(mixing, channels, axis=0)
        first_section = jnp.einsum("suma,sac->sumc", fetched.astype(jnp.float32), blocks.astype(jnp.float32)).astype(jnp.bfloat16)
        mixed_section = jnp.einsum("suv,sumc->svmc", mix_slots.astype(jnp.float32), first_section.astype(jnp.float32)).astype(jnp.bfloat16)
        split_blocks = blocks.astype(jnp.float32).reshape(BLK_SEC, N_ENV, row_count, M)
        split_mixed = mixed_section.astype(jnp.float32).reshape(BLK_SEC, W, N_ENV, row_count, M)
        partial_value = jnp.einsum("serc,sverd->evcd", split_blocks, split_mixed).astype(jnp.bfloat16)
        return jnp.sum(partial_value.astype(jnp.float32), axis=0).astype(jnp.bfloat16)

    return lax.map(one_sector, jnp.arange(NS, dtype=jnp.int32))


def reference(env_left, env_right, site_left, site_right, source_left, source_right, channel_left, channel_right, fanin_left, fanin_right, operator_table, operator_pattern):
    operator = (operator_table.astype(jnp.float32) * operator_pattern.astype(jnp.float32)).astype(jnp.bfloat16)
    new_left = side_rebuild(env_left, site_left, source_left, channel_left, fanin_left, operator)
    new_right = side_rebuild(env_right, site_right, source_right, channel_right, fanin_right, jnp.transpose(operator, (0, 2, 1)))
    return (new_left, new_right)
```

```python
import functools

import jax
import jax.numpy as jnp
from jax import lax
from jax.experimental import pallas as pl
from jax.experimental.pallas import tpu as pltpu
from jax.sharding import PartitionSpec as P

GROUP = 8


def side_kernel(
    dims, own_ref, ch_ref, sel_ref, fan_ref, pos_ref, mix_ref, env_ref, site_ref, *rest
):
    owners, ops, chans, rows, states, per_sec, secs, n_env = dims
    outs = rest[:n_env]
    e_buf, e_f32, mixed, x_buf, acc, site_buf, e_sem, s_sem = rest[n_env:]
    depth = GROUP * rows

    site_copy = pltpu.make_async_copy(site_ref, site_buf, s_sem)
    site_copy.start()

    def env_copy(o):
        return pltpu.make_async_copy(env_ref.at[sel_ref[o]], e_buf.at[o], e_sem.at[o])

    for o in range(owners):
        env_copy(o).start()

    def mix_owner(o, _):
        env_copy(o).wait()
        e_f32[...] = e_buf[o].astype(jnp.float32).reshape(chans * rows, states)
        for m in range(0, rows, 2):
            pair = jnp.concatenate(
                [e_f32[pl.ds(m + i, chans, stride=rows), :] for i in (0, 1)], axis=1
            ).astype(jnp.bfloat16)
            res = jnp.dot(mix_ref[...], pair, preferred_element_type=jnp.float32)
            for p in range(ops):
                part = res[p * chans : (p + 1) * chans]
                both = jnp.concatenate([part[:, :states], part[:, states:]], axis=0)
                mixed[o, p, m * chans : (m + 2) * chans, :] = both.astype(jnp.bfloat16)
        return 0

    lax.fori_loop(0, owners, mix_owner, 0)
    site_copy.wait()
    first_row = pl.multiple_of(pos_ref[0] * rows, rows)

    for k in range(secs):
        fan = fan_ref[k]
        acc[...] = jnp.zeros_like(acc)

        def group(g, _):
            base = k * per_sec + g * GROUP
            row_parts = []
            for t in range(0, GROUP, 2):
                j0, j1 = base + t, base + t + 1
                lhs = jnp.concatenate(
                    [mixed[own_ref[j0], ch_ref[j0]], mixed[own_ref[j1], ch_ref[j1]]], axis=1
                )
                zero = jnp.zeros((states, states), jnp.bfloat16)
                rhs = jnp.concatenate(
                    [
                        jnp.concatenate([site_buf[j0], zero], axis=1),
                        jnp.concatenate([zero, site_buf[j1]], axis=1),
                    ],
                    axis=0,
                )
                res = jnp.dot(lhs, rhs, preferred_element_type=jnp.float32)
                for i in (0, 1):
                    for m in range(rows):
                        x_buf[pl.ds((t + i) * rows + m, chans, stride=depth), :] = res[
                            m * chans : (m + 1) * chans, i * states : (i + 1) * states
                        ]
            for t in range(GROUP):
                piece = site_buf[base + t, pl.ds(first_row, rows), :].astype(jnp.float32)
                live = g * GROUP + t < fan
                row_parts.append(jnp.where(live, piece, 0.0))
            row_mat = jnp.concatenate(row_parts, axis=0).T.astype(jnp.bfloat16)
            for v in range(0, chans, 2):
                pair = jnp.concatenate(
                    [
                        x_buf[(v + i) * depth : (v + i + 1) * depth, :].astype(jnp.bfloat16)
                        for i in (0, 1)
                    ],
                    axis=1,
                )
                acc[:, v * states : (v + 2) * states] += jnp.dot(
                    row_mat, pair, preferred_element_type=jnp.float32
                )
            return 0

        lax.fori_loop(0, (fan + GROUP - 1) // GROUP, group, 0)
        for d in range(n_env):
            start = pl.multiple_of((pos_ref[0] ^ d) * rows, rows)
            for v in range(chans):
                outs[d][k, v] = acc[pl.ds(start, rows), v * states : (v + 1) * states].astype(
                    jnp.bfloat16
                )


def side_compute(gathered, site, own, ch, sel, fan, pos, mix_rows, n_env):
    chans, rows, states = gathered.shape[1:]
    secs = fan.shape[0]
    owners = sel.shape[0]
    slots = site.shape[0]
    ops = mix_rows.shape[0] // chans
    dims = (owners, ops, chans, rows, states, slots // secs, secs, n_env)
    smem = pl.BlockSpec(memory_space=pltpu.SMEM)
    vmem = pl.BlockSpec(memory_space=pltpu.VMEM)
    hbm = pl.BlockSpec(memory_space=pl.ANY)
    out = jax.ShapeDtypeStruct((secs, chans, rows, states), jnp.bfloat16)
    return pl.pallas_call(
        functools.partial(side_kernel, dims),
        out_shape=[out] * n_env,
        in_specs=[smem] * 5 + [vmem, hbm, hbm],
        out_specs=[vmem] * n_env,
        scratch_shapes=[
            pltpu.VMEM((owners, chans, rows, states), jnp.bfloat16),
            pltpu.VMEM((chans * rows, states), jnp.float32),
            pltpu.VMEM((owners, ops, rows * chans, states), jnp.bfloat16),
            pltpu.VMEM((chans * GROUP * rows, states), jnp.float32),
            pltpu.VMEM((states, chans * states), jnp.float32),
            pltpu.VMEM((slots, states, states), jnp.bfloat16),
            pltpu.SemaphoreType.DMA((owners,)),
            pltpu.SemaphoreType.DMA,
        ],
        compiler_params=pltpu.CompilerParams(vmem_limit_bytes=62 * 1024 * 1024),
    )(own, ch, sel, fan, pos, mix_rows, gathered, site)


def selection(source, owners, per_owner):
    ids = jnp.arange(owners, dtype=jnp.int32)
    own = source // per_owner
    hit = own[None, :] == ids[:, None]
    sel = jnp.max(jnp.where(hit, source[None, :], (ids * per_owner)[:, None]), axis=1)
    return own, sel


def rebuild(old, site, source, ch, fan, mix_rows, n_env):
    pos = lax.axis_index("env").astype(jnp.int32).reshape(1)
    owners = lax.axis_size("sec")
    own, sel = selection(source, owners, old.shape[0])
    gathered = lax.all_gather(old, "sec", axis=0, tiled=True)
    parts = side_compute(gathered, site, own, ch, sel, fan, pos, mix_rows, n_env)
    total = parts[0].astype(jnp.float32)
    for d in range(1, n_env):
        pairs = [(e, e ^ d) for e in range(n_env)]
        total += lax.ppermute(parts[d], "env", pairs).astype(jnp.float32)
    return total.astype(jnp.bfloat16)


def per_device(n_env, env_l, env_r, site_l, site_r, src_l, src_r, ch_l, ch_r, fan_l, fan_r, table, pattern):
    operator = table * pattern.astype(table.dtype)
    ops, chans = operator.shape[:2]
    mix_l = jnp.transpose(operator, (0, 2, 1)).reshape(ops * chans, chans)
    mix_r = operator.reshape(ops * chans, chans)
    new_l = rebuild(env_l, site_l, src_l, ch_l, fan_l, mix_l, n_env)
    new_r = rebuild(env_r, site_r, src_r, ch_r, fan_r, mix_r, n_env)
    return new_l, new_r


def solution(mesh):
    n_env = mesh.shape["env"]
    tile = P("sec", None, "env", None)
    block = P("sec", None, None)
    vec = P("sec")
    in_specs = (tile, tile, block, block, vec, vec, vec, vec, vec, vec, P(), P())
    return jax.shard_map(
        functools.partial(per_device, n_env),
        mesh=mesh,
        in_specs=in_specs,
        out_specs=(tile, tile),
        check_vma=False,
    )
```

```python
import functools

import jax
import jax.numpy as jnp
from jax import lax
from jax.experimental import pallas as pl
from jax.experimental.pallas import tpu as pltpu
from jax.sharding import PartitionSpec as P

GROUP = 8
PITCH = 1


def side_kernel(
    dims, own_ref, ch_ref, sel_ref, fan_ref, pos_ref, mix_ref, env_ref, site_ref, *rest
):
    owners, ops, chans, rows, states, per_sec, secs, n_env = dims
    outs = rest[:n_env]
    e_buf, e_f32, mixed, x_buf, acc, site_buf, e_sem, s_sem = rest[n_env:]
    depth = GROUP * rows

    site_copy = pltpu.make_async_copy(site_ref, site_buf, s_sem)
    site_copy.start()

    def env_copy(o):
        return pltpu.make_async_copy(env_ref.at[sel_ref[o]], e_buf.at[o], e_sem.at[o])

    for o in range(owners):
        env_copy(o).start()

    def mix_owner(o, _):
        env_copy(o).wait()
        for u in range(chans):
            e_f32[pl.ds(u * (rows + PITCH), rows), :] = e_buf[o, u].astype(jnp.float32)
        for m in range(0, rows, 2):
            pair = jnp.concatenate(
                [e_f32[pl.ds(m + i, chans, stride=rows + PITCH), :] for i in (0, 1)], axis=1
            ).astype(jnp.bfloat16)
            res = jnp.dot(mix_ref[...], pair, preferred_element_type=jnp.float32)
            for p in range(ops):
                part = res[p * chans : (p + 1) * chans]
                both = jnp.concatenate([part[:, :states], part[:, states:]], axis=0)
                mixed[o, p, m * chans : (m + 2) * chans, :] = both.astype(jnp.bfloat16)
        return 0

    lax.fori_loop(0, owners, mix_owner, 0)
    site_copy.wait()
    first_row = pl.multiple_of(pos_ref[0] * rows, rows)

    for k in range(secs):
        fan = fan_ref[k]
        acc[...] = jnp.zeros_like(acc)

        def group(g, _):
            base = k * per_sec + g * GROUP
            row_parts = []
            for t in range(0, GROUP, 2):
                j0, j1 = base + t, base + t + 1
                lhs = jnp.concatenate(
                    [mixed[own_ref[j0], ch_ref[j0]], mixed[own_ref[j1], ch_ref[j1]]], axis=1
                )
                zero = jnp.zeros((states, states), jnp.bfloat16)
                rhs = jnp.concatenate(
                    [
                        jnp.concatenate([site_buf[j0], zero], axis=1),
                        jnp.concatenate([zero, site_buf[j1]], axis=1),
                    ],
                    axis=0,
                )
                res = jnp.dot(lhs, rhs, preferred_element_type=jnp.float32)
                for i in (0, 1):
                    for m in range(rows):
                        x_buf[pl.ds((t + i) * rows + m, chans, stride=depth + PITCH), :] = res[
                            m * chans : (m + 1) * chans, i * states : (i + 1) * states
                        ]
            for t in range(GROUP):
                piece = site_buf[base + t, pl.ds(first_row, rows), :].astype(jnp.float32)
                live = g * GROUP + t < fan
                row_parts.append(jnp.where(live, piece, 0.0))
            row_mat = jnp.concatenate(row_parts, axis=0).T.astype(jnp.bfloat16)
            for v in range(0, chans, 2):
                pair = jnp.concatenate(
                    [
                        x_buf[pl.ds((v + i) * (depth + PITCH), depth), :].astype(jnp.bfloat16)
                        for i in (0, 1)
                    ],
                    axis=1,
                )
                acc[:, v * states : (v + 2) * states] += jnp.dot(
                    row_mat, pair, preferred_element_type=jnp.float32
                )
            return 0

        lax.fori_loop(0, (fan + GROUP - 1) // GROUP, group, 0)
        for d in range(n_env):
            start = pl.multiple_of((pos_ref[0] ^ d) * rows, rows)
            for v in range(chans):
                outs[d][k, v] = acc[pl.ds(start, rows), v * states : (v + 1) * states].astype(
                    jnp.bfloat16
                )


def side_compute(gathered, site, own, ch, sel, fan, pos, mix_rows, n_env):
    chans, rows, states = gathered.shape[1:]
    secs = fan.shape[0]
    owners = sel.shape[0]
    slots = site.shape[0]
    ops = mix_rows.shape[0] // chans
    dims = (owners, ops, chans, rows, states, slots // secs, secs, n_env)
    smem = pl.BlockSpec(memory_space=pltpu.SMEM)
    vmem = pl.BlockSpec(memory_space=pltpu.VMEM)
    hbm = pl.BlockSpec(memory_space=pl.ANY)
    out = jax.ShapeDtypeStruct((secs, chans, rows, states), jnp.bfloat16)
    return pl.pallas_call(
        functools.partial(side_kernel, dims),
        out_shape=[out] * n_env,
        in_specs=[smem] * 5 + [vmem, hbm, hbm],
        out_specs=[vmem] * n_env,
        scratch_shapes=[
            pltpu.VMEM((owners, chans, rows, states), jnp.bfloat16),
            pltpu.VMEM((chans * (rows + PITCH), states), jnp.float32),
            pltpu.VMEM((owners, ops, rows * chans, states), jnp.bfloat16),
            pltpu.VMEM((chans * (GROUP * rows + PITCH), states), jnp.float32),
            pltpu.VMEM((states, chans * states), jnp.float32),
            pltpu.VMEM((slots, states, states), jnp.bfloat16),
            pltpu.SemaphoreType.DMA((owners,)),
            pltpu.SemaphoreType.DMA,
        ],
        compiler_params=pltpu.CompilerParams(vmem_limit_bytes=62 * 1024 * 1024),
    )(own, ch, sel, fan, pos, mix_rows, gathered, site)


def selection(source, owners, per_owner):
    ids = jnp.arange(owners, dtype=jnp.int32)
    own = source // per_owner
    hit = own[None, :] == ids[:, None]
    sel = jnp.max(jnp.where(hit, source[None, :], (ids * per_owner)[:, None]), axis=1)
    return own, sel


def rebuild(old, site, source, ch, fan, mix_rows, n_env):
    pos = lax.axis_index("env").astype(jnp.int32).reshape(1)
    owners = lax.axis_size("sec")
    own, sel = selection(source, owners, old.shape[0])
    gathered = lax.all_gather(old, "sec", axis=0, tiled=True)
    parts = side_compute(gathered, site, own, ch, sel, fan, pos, mix_rows, n_env)
    total = parts[0].astype(jnp.float32)
    for d in range(1, n_env):
        pairs = [(e, e ^ d) for e in range(n_env)]
        total += lax.ppermute(parts[d], "env", pairs).astype(jnp.float32)
    return total.astype(jnp.bfloat16)


def per_device(n_env, env_l, env_r, site_l, site_r, src_l, src_r, ch_l, ch_r, fan_l, fan_r, table, pattern):
    operator = table * pattern.astype(table.dtype)
    ops, chans = operator.shape[:2]
    mix_l = jnp.transpose(operator, (0, 2, 1)).reshape(ops * chans, chans)
    mix_r = operator.reshape(ops * chans, chans)
    new_l = rebuild(env_l, site_l, src_l, ch_l, fan_l, mix_l, n_env)
    new_r = rebuild(env_r, site_r, src_r, ch_r, fan_r, mix_r, n_env)
    return new_l, new_r


def solution(mesh):
    n_env = mesh.shape["env"]
    tile = P("sec", None, "env", None)
    block = P("sec", None, None)
    vec = P("sec")
    in_specs = (tile, tile, block, block, vec, vec, vec, vec, vec, vec, P(), P())
    return jax.shard_map(
        functools.partial(per_device, n_env),
        mesh=mesh,
        in_specs=in_specs,
        out_specs=(tile, tile),
        check_vma=False,
    )
```
